128 devices in a mesh: req: 4 (over y), seq: 32 (over x, z, core).
Axes of the slice: x: 4, y: 4, z: 4, core: 2. Of those that a mesh axis runs over, the one named last changes fastest.
Arguments:
- inputs: bfloat16 [1, 32, 5120], P(None, 'req', 'seq'), may hold values from -6 to 6
- lengths: int32 [32], P('req'), may hold values from 4 to 4096, as said below
- targets: int32 [1, 32], replicated, may hold values from 0 to 81919
- cache_keys: bfloat16 [32, 4096, 8, 128], P('req', 'seq'), may hold values from -192 to 192
- cache_values: bfloat16 [32, 4096, 8, 128], P('req', 'seq'), may hold values from -30 to 30
- attention_gain: float32 [5120], replicated, may hold values from 0.1 to 1.9
- packed_weight: bfloat16 [5120, 7168], P(None, 'seq'), may hold values from -0.078125 to 0.078125
- packed_bias: float32 [7168], P('seq'), may hold values from -3 to 3
- out_weight: bfloat16 [5120, 5120], P(None, 'seq'), may hold values from -0.078125 to 0.078125
- feedforward_gain: float32 [5120], replicated, may hold values from 0.1 to 1.9
- gate_weight: bfloat16 [5120, 27648], P(None, ('req', 'seq')), may hold values from -0.078125 to 0.078125
- up_weight: bfloat16 [5120, 27648], P(None, ('req', 'seq')), may hold values from -0.078125 to 0.078125
- down_weight: bfloat16 [27648, 5120], P(('req', 'seq')), may hold values from -0.125 to 0.125
- final_gain: float32 [5120], replicated, may hold values from 0.1 to 1.9
- head_weight: bfloat16 [5120, 81920], P(None, ('req', 'seq')), may hold values from -7.5467294 to 7.5467294
Outputs:
- hidden_states: bfloat16 [1, 32, 5120], P(None, 'req', 'seq')
- log_probs: float32 [1, 32], replicated
The draws below stay inside these ranges and needn't reach their ends.
Inputs may be any that keep to these rules, and one draw needn't show every extreme that they name: Every draw has a request with exactly 4096 cached positions; lengths are spread evenly in the logarithm.
All inputs are finite; a program needn't handle non-finite values.
Results may differ from the reference program's by a relative error of at most 0.013.
Values may be sent and summed in bfloat16 or wider, within the bound.
A program may use at most 128 MiB of HBM per device.

```python
import jax
import jax.numpy as jnp
from jax import lax

D = 5120
HEAD_DIM = 128
Q_HEADS = 40
KV_HEADS = 8
FF = 27648
VOCAB = 81920
MAXLEN = 4096
STEPS = 1
REQUESTS = 32
QKV_WIDTH = 7168


def draw_lengths(key, part):
    top_power = int(MAXLEN).bit_length() - 1
    key_one, key_two, key_three = jax.random.split(key, 3)
    exponent = jax.random.randint(key_one, (REQUESTS,), 2, top_power + 1)
    base_value = jnp.left_shift(jnp.ones((REQUESTS,), jnp.int32), exponent)
    offset = jax.random.randint(key_two, (REQUESTS,), 0, 1 << 30) % base_value
    drawn = jnp.minimum(base_value + offset, MAXLEN)
    longest = jax.random.randint(key_three, (), 0, REQUESTS)
    return jnp.where(jnp.arange(REQUESTS) == longest, MAXLEN, drawn).astype(jnp.int32)


def draw_cache_keys(key, part):
    values = jnp.clip(jax.random.normal(key, (REQUESTS, MAXLEN, KV_HEADS, HEAD_DIM), jnp.float32), -6.0, 6.0)
    return values.astype(jnp.bfloat16)


def draw_cache_values(key, part):
    key_noise = jax.random.fold_in(key, 21)
    key_mean = jax.random.fold_in(key, 22)
    ramp = jnp.arange(MAXLEN, dtype=jnp.float32) / MAXLEN
    noise = jnp.clip(jax.random.normal(key_noise, (REQUESTS, MAXLEN, KV_HEADS, HEAD_DIM), jnp.float32), -6.0, 6.0)
    common = jnp.clip(jax.random.normal(key_mean, (REQUESTS, 1, KV_HEADS, HEAD_DIM), jnp.float32), -2.5, 2.5)
    factor = 1.0 + 2.0 * ramp
    values = noise + common * factor[None, :, None, None]
    return values.astype(jnp.bfloat16)


def draw_head_weight(key, part):
    values = jnp.clip(jax.random.normal(key, (D, VOCAB), jnp.float32), -6.0, 6.0) * (3.0 * D ** (-0.5))
    return values.astype(jnp.bfloat16)


def place_ends(entries, rng, least, high):
    longest = entries.shape.index(max(entries.shape))
    spots = []
    for shift in (0, 1):
        where = [jax.random.randint(jax.random.fold_in(rng, axis), (), 0, length) for axis, length in enumerate(entries.shape)]
        where[longest] = (where[longest] + shift) % entries.shape[longest]
        spots.append(tuple(where))
    return entries.at[spots[0]].set(least).at[spots[1]].set(high)


def strengthened(values, own_key, source, target, parts, factor):
    def block_of(dim):
        return (jnp.arange(values.shape[dim]) // (values.shape[dim] // parts)).reshape((-1,) + (1,) * (values.ndim - 1 - dim))

    one_side = jax.random.permutation(own_key, parts)[block_of(target)]
    far = (block_of(target) + parts // 2) % parts
    return jnp.where((block_of(source) == one_side) | (block_of(source) == far), factor * values, values)


def levels(key, dims, cuts, low, top_value):
    factor_of = 1.0
    for axis_at, shards_of in cuts:
        heights = jax.random.uniform(jax.random.fold_in(jax.random.fold_in(key, 6), axis_at), (shards_of,), jnp.float32, low / len(cuts), top_value / len(cuts))
        factor_of = factor_of * jnp.repeat(jnp.exp(heights), dims[axis_at] // shards_of).reshape((-1,) + (1,) * (len(dims) - 1 - axis_at))
    return factor_of


def gaussian(own_key, dims, spread, most, pieces=(), held_as=jnp.bfloat16):
    loudness = levels(own_key, dims, pieces, -0.22, 0.18) if pieces else 1.0
    array = jax.random.normal(own_key, dims, jnp.float32) * spread * loudness
    return jnp.minimum(jnp.maximum(array, -most), most).astype(held_as)


def bell_draw_with(key, shape, width, most, cuts, heavy, kind=jnp.bfloat16):
    array = width * jax.random.normal(key, shape, jnp.float32)
    if cuts:
        array = array * levels(key, shape, cuts, -0.22, 0.18)
    return jnp.clip(strengthened(array, jax.random.fold_in(key, 3), *heavy), -most, most).astype(kind)


def setup_inputs(seed: int = 0) -> dict:
    streams_of = jax.random.split(jax.random.key(seed), 16)
    inputs = gaussian(streams_of[0], (STEPS, REQUESTS, D), 1.0, 6.0, ((1, 4), (2, 32)))
    lengths = draw_lengths(jax.random.fold_in(streams_of[15], 71), 0)
    targets = place_ends(jax.random.randint(streams_of[2], (STEPS, REQUESTS), 0, VOCAB), jax.random.fold_in(streams_of[2], 1), 0, VOCAB - 1).astype(jnp.int32)
    cache_keys = draw_cache_keys(jax.random.fold_in(streams_of[15], 71), 0)
    cache_values = draw_cache_values(jax.random.fold_in(streams_of[15], 71), 0)
    attention_gain = jnp.clip(1.0 + 0.18 * jax.random.normal(streams_of[5], (D,), jnp.float32), 0.1, 1.9)
    packed_weight = gaussian(streams_of[6], (D, QKV_WIDTH), D ** -0.5, 0.078125, ((1, 32),))
    packed_bias = gaussian(streams_of[7], (QKV_WIDTH,), 0.5, 3.0, ((0, 32),), jnp.float32)
    out_weight = gaussian(streams_of[8], (D, D), D ** -0.5, 0.078125, ((1, 32),))
    feedforward_gain = jnp.clip(1.0 + 0.18 * jax.random.normal(streams_of[9], (D,), jnp.float32), 0.1, 1.9)
    gate_weight = gaussian(streams_of[10], (D, FF), D ** -0.5, 0.078125, ((1, 128),))
    up_weight = gaussian(streams_of[11], (D, FF), D ** -0.5, 0.078125, ((1, 128),))
    down_weight = bell_draw_with(streams_of[12], (FF, D), FF ** -0.5, 0.125, ((0, 128),), (0, 1, 128, 5.5))
    final_gain = jnp.clip(1.0 + 0.18 * jax.random.normal(streams_of[13], (D,), jnp.float32), 0.1, 1.9)
    head_weight = draw_head_weight(jax.random.fold_in(streams_of[15], 71), 0)
    return dict(inputs=inputs, lengths=lengths, targets=targets, cache_keys=cache_keys, cache_values=cache_values, attention_gain=attention_gain, packed_weight=packed_weight, packed_bias=packed_bias, out_weight=out_weight, feedforward_gain=feedforward_gain, gate_weight=gate_weight, up_weight=up_weight, down_weight=down_weight, final_gain=final_gain, head_weight=head_weight)


EPSILON = 1e-06
THETA = 1000000.0

def normalize(values, gain_vector):
    wide = values.astype(jnp.float32)
    return wide * lax.rsqrt(lax.optimization_barrier(jnp.mean(wide * wide, axis=-1, keepdims=True)) + EPSILON) * gain_vector

def rotate(vectors, position):
    half_dim = vectors.shape[-1] // 2
    inverse = THETA ** (-(jnp.arange(half_dim, dtype=jnp.float32) * 2.0 / vectors.shape[-1]))
    angle = position[..., None] * inverse
    cosine = jnp.cos(angle)
    sine = jnp.sin(angle)
    first_half = vectors[..., :half_dim]
    second_half = vectors[..., half_dim:]
    return jnp.concatenate([first_half * cosine - second_half * sine, second_half * cosine + first_half * sine], axis=-1)

def reference(inputs, lengths, targets, cache_keys, cache_values, attention_gain, packed_weight, packed_bias, out_weight, feedforward_gain, gate_weight, up_weight, down_weight, final_gain, head_weight):
    group_size = Q_HEADS // KV_HEADS
    scale_factor = HEAD_DIM ** (-0.5)
    query_width = Q_HEADS * HEAD_DIM
    key_width = KV_HEADS * HEAD_DIM
    keys_wide = cache_keys.astype(jnp.float32)
    values_wide = cache_values.astype(jnp.float32)
    cached_live = jnp.arange(MAXLEN, dtype=jnp.int32)[None, :] < lengths[:, None]
    new_keys = []
    new_values = []
    states = []
    probabilities = []
    for step_index in range(STEPS):
        current = inputs[step_index]
        normed = normalize(current, attention_gain).astype(jnp.bfloat16)
        packed = (jnp.dot(normed, packed_weight, preferred_element_type=jnp.float32) + packed_bias).astype(jnp.bfloat16)
        position = (lengths + step_index).astype(jnp.float32)[:, None]
        query = rotate(packed[:, :query_width].astype(jnp.float32).reshape(REQUESTS, Q_HEADS, HEAD_DIM), position).astype(jnp.bfloat16)
        key_now = rotate(packed[:, query_width:query_width + key_width].astype(jnp.float32).reshape(REQUESTS, KV_HEADS, HEAD_DIM), position).astype(jnp.bfloat16)
        new_keys.append(key_now)
        new_values.append(packed[:, query_width + key_width:].reshape(REQUESTS, KV_HEADS, HEAD_DIM))
        grouped = query.astype(jnp.float32).reshape(REQUESTS, KV_HEADS, group_size, HEAD_DIM)
        cache_scores = jnp.einsum('rkjd,rpkd->rkjp', grouped, keys_wide) * scale_factor
        cache_scores = jnp.where(cached_live[:, None, None, :], cache_scores, -jnp.inf)
        recent_keys = jnp.stack(new_keys, axis=1).astype(jnp.float32)
        recent_values = jnp.stack(new_values, axis=1).astype(jnp.float32)
        recent_scores = jnp.einsum('rkjd,rukd->rkju', grouped, recent_keys) * scale_factor
        top_score = jnp.maximum(cache_scores.max(axis=-1), recent_scores.max(axis=-1))
        cache_weights = jnp.exp(cache_scores - top_score[..., None]).astype(jnp.bfloat16).astype(jnp.float32)
        recent_weights = jnp.exp(recent_scores - top_score[..., None]).astype(jnp.bfloat16).astype(jnp.float32)
        total = cache_weights.sum(axis=-1) + recent_weights.sum(axis=-1)
        summed = jnp.einsum('rkjp,rpkd->rkjd', cache_weights, values_wide) + jnp.einsum('rkju,rukd->rkjd', recent_weights, recent_values)
        attention = (summed / total[..., None]).reshape(REQUESTS, query_width).astype(jnp.bfloat16)
        mixed = (current.astype(jnp.float32) + jnp.dot(attention, out_weight, preferred_element_type=jnp.float32)).astype(jnp.bfloat16)
        normed = normalize(mixed, feedforward_gain).astype(jnp.bfloat16)
        gate_part = jnp.dot(normed, gate_weight, preferred_element_type=jnp.float32)
        up_part = jnp.dot(normed, up_weight, preferred_element_type=jnp.float32)
        hidden = (jax.nn.silu(gate_part) * up_part).astype(jnp.bfloat16)
        result = (mixed.astype(jnp.float32) + jnp.dot(hidden, down_weight, preferred_element_type=jnp.float32)).astype(jnp.bfloat16)
        states.append(result)
        normed = normalize(result, final_gain).astype(jnp.bfloat16)
        logits = jnp.dot(normed, head_weight, preferred_element_type=jnp.float32)
        largest = logits.max(axis=-1)
        log_total = largest + jnp.log(lax.optimization_barrier(jnp.sum(jnp.exp(logits - largest[:, None]), axis=-1)))
        picked = jnp.take_along_axis(logits, targets[step_index][:, None], axis=1)[:, 0]
        probabilities.append(picked - log_total)
    return (jnp.stack(states), jnp.stack(probabilities))
```

```python
import functools

import jax
import jax.numpy as jnp
from jax import lax
from jax.experimental import pallas as pl
from jax.experimental.pallas import tpu as pltpu
from jax.sharding import PartitionSpec as P

EPSILON = 1e-06
THETA = 1000000.0
NEGATIVE = -1e30
MESH = pl.DeviceIdType.MESH
F32 = jnp.float32
BF16 = jnp.bfloat16

REQS = 4
SEQS = 32
ROWS = 8
ALL_ROWS = REQS * ROWS
HEADS = 40
KV = 8
GROUP = HEADS // KV
HEAD = 128
WIDTH = 5120
PART = WIDTH // SEQS
PACKED = 7168
PACKED_PART = PACKED // SEQS
FF_PART = 216
VOCAB_PART = 640
POSITIONS = 128
OWNERS = 20
SLAB = ROWS * HEADS // OWNERS
COLUMNS = WIDTH // OWNERS
SCALE = HEAD**-0.5


def owner_seq(index):
    late = index // 16
    return (1 - late) * 2 * index + late * (10 * (index - 16) + 1)


def matmul_nt(left, right):
    return lax.dot_general(left, right, (((1,), (1,)), ((), ())), preferred_element_type=F32)


def normalized(wide, gain):
    mean = jnp.mean(wide * wide, axis=-1, keepdims=True)
    return (wide * lax.rsqrt(mean + EPSILON) * gain).astype(BF16)


def kernel(
    lengths, targets, x_hbm, keys_hbm, values_hbm, gain1_hbm, packed_hbm, bias_hbm, out_hbm, gain2_hbm,
    gate_hbm, up_hbm, down_hbm, gain3_hbm, head_hbm,
    states_ref, probs_ref,
    keys, values, gain1, packed_w, bias, out_w, gain2, gate_w, up_w, down_w, gain3, head_w,
    xg, big, normed, pk, pkf, qs, kx, vx, of, sf, obuf, orecv, lse_s, ag, af, mg, fs, frecv, yex, rg, st, sh,
    load_sem, send_sem, recv_sem,
):
    me_req = lax.axis_index("req")
    me = lax.axis_index("seq")
    core = lax.rem(me, 2)
    chip = me // 2
    is_owner = (core == 0) | (lax.rem(chip, 5) == 0)
    mine = (1 - core) * chip + core * (16 + chip // 5)

    loads = []
    for index, (src, dst) in enumerate(
        [
            (x_hbm.at[0], xg.at[me]),
            (gain1_hbm, gain1),
            (bias_hbm, bias),
            (packed_hbm, packed_w),
            (keys_hbm, keys),
            (values_hbm, values),
            (out_hbm, out_w),
            (gain2_hbm, gain2),
            (gate_hbm, gate_w),
            (up_hbm, up_w),
            (down_hbm, down_w),
            (gain3_hbm, gain3),
            (head_hbm, head_w),
        ]
    ):
        copy = pltpu.make_async_copy(src, dst, load_sem.at[index])
        copy.start()
        loads.append(copy)

    barrier = pltpu.get_barrier_semaphore()

    def greet(step, carry):
        peer = lax.rem(me + step, SEQS)
        pl.semaphore_signal(barrier, inc=1, device_id={"seq": peer}, device_id_type=MESH)
        return carry

    lax.fori_loop(1, SEQS, greet, 0)
    for step in range(1, REQS):
        peer = lax.rem(me_req + step, REQS)
        pl.semaphore_signal(barrier, inc=1, device_id={"req": peer}, device_id_type=MESH)
    pl.semaphore_wait(barrier, SEQS - 1 + REQS - 1)

    def remote(src, dst, phase, where):
        return pltpu.make_async_remote_copy(
            src_ref=src,
            dst_ref=dst,
            send_sem=send_sem.at[phase],
            recv_sem=recv_sem.at[phase],
            device_id=where,
            device_id_type=MESH,
        )

    def to_seq(src, dst, phase):
        def body(step, carry):
            remote(src, dst, phase, {"seq": lax.rem(me + step, SEQS)}).start()
            return carry

        lax.fori_loop(1, SEQS, body, 0)

    def to_req(src, dst, phase):
        for step in range(1, REQS):
            remote(src, dst, phase, {"req": lax.rem(me_req + step, REQS)}).start()

    def to_owners(src_of, dst, phase, own_sem):
        def body(step, carry):
            index = lax.rem(me + step, OWNERS)
            peer = owner_seq(index)

            @pl.when(peer != me)
            def _():
                remote(src_of(index), dst, phase, {"seq": peer}).start()

            @pl.when(peer == me)
            def _():
                pltpu.make_async_copy(src_of(index), dst, own_sem).start()

            return carry

        lax.fori_loop(0, OWNERS, body, 0)

    def drain(ref, sem):
        pltpu.make_async_copy(ref, ref, sem).wait()

    to_seq(x_hbm.at[0], xg.at[me], 0)

    inverse = jnp.exp(
        lax.rem(lax.broadcasted_iota(jnp.int32, (ROWS, HEAD), 1), HEAD // 2).astype(F32)
        * (-2.0 / HEAD * 13.815510557964274)
    )
    row_ids = lax.broadcasted_iota(jnp.int32, (ROWS, HEAD), 0)
    position = jnp.zeros((ROWS, HEAD), jnp.int32)
    for row in range(ROWS):
        position = jnp.where(row_ids == row, lengths[row], position)
    angle = position.astype(F32) * inverse
    lane = lax.broadcasted_iota(jnp.int32, (ROWS, HEAD), 1)
    cosine = jnp.cos(angle)
    sine = jnp.sin(angle)
    signed_sine = jnp.where(lane < HEAD // 2, -sine, sine)

    loads[0].wait()
    drain(xg.at[pl.ds(0, SEQS - 1)], recv_sem.at[0])
    for part in range(SEQS):
        big[0:ROWS, PART * part : PART * (part + 1)] = xg[part].astype(F32)
    loads[1].wait()
    normed[0:ROWS, :] = normalized(big[0:ROWS, :], gain1[...])
    loads[2].wait()
    loads[3].wait()
    pk[me] = (matmul_nt(normed[0:ROWS, :], packed_w[...]) + bias[...]).astype(BF16)

    to_seq(pk.at[me], pk.at[me], 1)
    drain(pk.at[pl.ds(0, SEQS - 1)], recv_sem.at[1])
    for part in range(SEQS):
        pkf[:, PACKED_PART * part : PACKED_PART * (part + 1)] = pk[part].astype(F32)

    def rotated(column):
        head = pkf[:, HEAD * column : HEAD * (column + 1)]
        turned = head * cosine + pltpu.roll(head, HEAD // 2, 1) * signed_sine
        return turned.astype(BF16).astype(F32)

    for head in range(HEADS):
        qs[pl.ds(head, ROWS, stride=HEADS), :] = rotated(head)

    loads[4].wait()
    loads[5].wait()
    column = lax.broadcasted_iota(jnp.int32, (HEADS, POSITIONS * KV), 1)
    line = lax.broadcasted_iota(jnp.int32, (HEADS, POSITIONS * KV), 0)
    same = lax.rem(column, KV) == line // GROUP
    spot = me * POSITIONS + column // KV
    place = jnp.where(same, spot, jnp.int32(1 << 30))
    for row in range(ROWS):
        query = qs[HEADS * row : HEADS * (row + 1), :].astype(BF16)
        scores = matmul_nt(query, keys[row]) * SCALE
        live = place < lengths[row]
        scores = jnp.where(live, scores, NEGATIVE)
        top = jnp.max(scores, axis=-1, keepdims=True)
        weights = jnp.where(live, jnp.exp(scores - top), 0.0).astype(BF16)
        total = jnp.sum(weights.astype(F32), axis=-1, keepdims=True)
        summed = jnp.dot(weights, values[row], preferred_element_type=F32)
        some = total > 0.0
        of[HEADS * row : HEADS * (row + 1), :] = summed / jnp.where(some, total, 1.0)
        lse = jnp.where(some, top + jnp.log(jnp.where(some, total, 1.0)), NEGATIVE)
        sf[HEADS * row : HEADS * (row + 1), :] = jnp.broadcast_to(lse, (HEADS, HEAD))

    slab_lane = lax.broadcasted_iota(jnp.int32, (SLAB, HEAD), 1)
    for index in range(OWNERS):
        obuf[index, :, 0:HEAD] = of[SLAB * index : SLAB * (index + 1), :].astype(BF16)
        lse = sf[SLAB * index : SLAB * (index + 1), :]
        high = lse.astype(BF16).astype(F32)
        middle = (lse - high).astype(BF16).astype(F32)
        low = lse - high - middle
        packed_lse = jnp.where(
            slab_lane == 0, high, jnp.where(slab_lane == 1, middle, jnp.where(slab_lane == 2, low, 0.0))
        )
        obuf[index, :, HEAD : 2 * HEAD] = packed_lse.astype(BF16)

    to_owners(lambda index: obuf.at[index], orecv.at[me], 2, load_sem.at[13])

    for head in range(KV):
        new_key = rotated(HEADS + head)
        new_value = pkf[:, HEAD * (HEADS + KV + head) : HEAD * (HEADS + KV + head + 1)]
        for inner in range(GROUP):
            kx[pl.ds(GROUP * head + inner, ROWS, stride=HEADS), :] = new_key
            vx[pl.ds(GROUP * head + inner, ROWS, stride=HEADS), :] = new_value

    @pl.when(is_owner)
    def _():
        lines = pl.ds(pl.multiple_of(mine * SLAB, SLAB), SLAB)
        fresh = jnp.sum(qs[lines, :] * kx[lines, :], axis=-1, keepdims=True) * SCALE
        pltpu.make_async_copy(obuf.at[mine], orecv.at[me], load_sem.at[13]).wait()
        drain(orecv.at[pl.ds(0, SEQS - 1)], recv_sem.at[2])
        top = jnp.broadcast_to(fresh, (SLAB, HEAD))
        for part in range(SEQS):
            lse = jnp.sum(orecv[part, :, HEAD : 2 * HEAD].astype(F32), axis=-1, keepdims=True)
            lse = jnp.broadcast_to(lse, (SLAB, HEAD))
            lse_s[part] = lse
            top = jnp.maximum(top, lse)
        share = jnp.exp(fresh - top)
        total = share
        summed = share * vx[lines, :]
        for part in range(SEQS):
            share = jnp.exp(lse_s[part] - top)
            total = total + share
            summed = summed + share * orecv[part, :, 0:HEAD].astype(F32)
        ag[mine] = (summed / total).astype(BF16)
        to_seq(ag.at[mine], ag.at[mine], 3)
        drain(ag.at[pl.ds(0, OWNERS - 1)], recv_sem.at[3])

    @pl.when(jnp.logical_not(is_owner))
    def _():
        drain(ag, recv_sem.at[3])

    for index in range(OWNERS):
        af[SLAB * index : SLAB * (index + 1), :] = ag[index].astype(F32)
    for head in range(HEADS):
        normed[0:ROWS, HEAD * head : HEAD * (head + 1)] = af[pl.ds(head, ROWS, stride=HEADS), :].astype(BF16)
    loads[6].wait()
    mixed = xg[me].astype(F32) + matmul_nt(normed[0:ROWS, :], out_w[...])
    mg[me, me_req] = mixed.astype(BF16)

    to_req(mg.at[me, me_req], mg.at[me, me_req], 4)
    drain(mg.at[0, pl.ds(0, REQS - 1)], recv_sem.at[4])
    to_seq(mg.at[me], mg.at[me], 5)
    drain(mg.at[pl.ds(0, SEQS - 1)], recv_sem.at[5])
    for part in range(SEQS):
        for group in range(REQS):
            big[ROWS * group : ROWS * (group + 1), PART * part : PART * (part + 1)] = mg[part, group].astype(F32)
    loads[7].wait()
    normed[...] = normalized(big[...], gain2[...])
    loads[8].wait()
    gate = matmul_nt(normed[...], gate_w[...])
    loads[9].wait()
    up = matmul_nt(normed[...], up_w[...])
    hidden = (gate / (1.0 + jnp.exp(-gate)) * up).astype(BF16)
    loads[10].wait()
    for index in range(OWNERS):
        fs[index] = jnp.dot(
            hidden, down_w[:, COLUMNS * index : COLUMNS * (index + 1)], preferred_element_type=F32
        ).astype(BF16)

    to_owners(lambda index: fs.at[index], frecv.at[me], 6, load_sem.at[14])

    @pl.when(is_owner)
    def _():
        pltpu.make_async_copy(fs.at[mine], frecv.at[me], load_sem.at[14]).wait()
        drain(frecv.at[pl.ds(0, SEQS - 1)], recv_sem.at[6])
        partial = frecv[0].astype(F32)
        for part in range(1, SEQS):
            partial = partial + frecv[part].astype(F32)
        yex[me_req] = partial
        to_req(yex.at[me_req], yex.at[me_req], 7)
        drain(yex.at[pl.ds(0, REQS - 1)], recv_sem.at[7])
        feed = yex[0] + yex[1] + yex[2] + yex[3]
        columns = pl.ds(pl.multiple_of(mine * COLUMNS, COLUMNS), COLUMNS)
        rg[mine] = (big[:, columns] + feed).astype(BF16)
        to_seq(rg.at[mine], rg.at[mine], 8)
        drain(rg.at[pl.ds(0, OWNERS - 1)], recv_sem.at[8])

    @pl.when(jnp.logical_not(is_owner))
    def _():
        drain(rg, recv_sem.at[8])

    for index in range(OWNERS):
        big[:, COLUMNS * index : COLUMNS * (index + 1)] = rg[index].astype(F32)
    tile = (me * PART) // HEAD
    window = big[
        pl.ds(pl.multiple_of(me_req * ROWS, ROWS), ROWS), pl.ds(pl.multiple_of(tile * HEAD, HEAD), 2 * HEAD)
    ]
    block = window
    for quarter in range(1, 4):
        block = jnp.where(lax.rem(me, 4) == quarter, pltpu.roll(window, 256 - 32 * quarter, 1), block)
    states_ref[0] = block[:, 0:PART].astype(BF16)

    loads[11].wait()
    normed[...] = normalized(big[...], gain3[...])
    loads[12].wait()
    logits = jnp.dot(normed[...], head_w[...], preferred_element_type=F32)
    ids = (me_req * SEQS + me) * VOCAB_PART + lax.broadcasted_iota(jnp.int32, (ALL_ROWS, VOCAB_PART), 1)
    rows = lax.broadcasted_iota(jnp.int32, (ALL_ROWS, HEAD), 0)
    wanted = jnp.zeros((ALL_ROWS, HEAD), jnp.int32)
    for row in range(ALL_ROWS):
        wanted = jnp.where(rows == row, targets[0, row], wanted)
    picked = jnp.sum(jnp.where(ids == wanted[:, 0:1], logits, 0.0), axis=-1, keepdims=True)
    top = jnp.max(logits, axis=-1, keepdims=True)
    total = jnp.sum(jnp.exp(logits - top), axis=-1, keepdims=True)
    lanes = lax.broadcasted_iota(jnp.int32, (ALL_ROWS, HEAD), 1)
    stats = jnp.where(lanes == 0, top, jnp.where(lanes == 1, total, jnp.where(lanes == 2, picked, 0.0)))
    stats = jnp.concatenate([stats, jnp.zeros((HEAD - ALL_ROWS, HEAD), F32)], axis=0)
    st[me_req] = stats.T[0:8, :]

    to_req(st.at[me_req], st.at[me_req], 9)
    drain(st.at[pl.ds(0, REQS - 1)], recv_sem.at[9])

    def joined(ref):
        tops, totals, picks = ref[:, 0, :], ref[:, 1, :], ref[:, 2, :]
        highest = jnp.max(tops, axis=0, keepdims=True)
        whole = jnp.sum(totals * jnp.exp(tops - highest), axis=0, keepdims=True)
        return highest, whole, jnp.sum(picks, axis=0, keepdims=True)

    highest, whole, pick = joined(st)
    sub = lax.broadcasted_iota(jnp.int32, (8, HEAD), 0)
    sh[me] = jnp.where(sub == 0, highest, jnp.where(sub == 1, whole, pick))
    to_seq(sh.at[me], sh.at[me], 10)
    drain(sh.at[pl.ds(0, SEQS - 1)], recv_sem.at[10])
    highest, whole, pick = joined(sh)
    probs_ref[...] = (pick - (highest + jnp.log(whole)))[:, 0:ALL_ROWS]

    drain(xg.at[pl.ds(0, SEQS - 1)], send_sem.at[0])
    drain(pk.at[pl.ds(0, SEQS - 1)], send_sem.at[1])
    drain(mg.at[0, pl.ds(0, REQS - 1)], send_sem.at[4])
    drain(mg.at[pl.ds(0, SEQS - 1)], send_sem.at[5])
    drain(st.at[pl.ds(0, REQS - 1)], send_sem.at[9])
    drain(sh.at[pl.ds(0, SEQS - 1)], send_sem.at[10])

    @pl.when(is_owner)
    def _():
        drain(obuf.at[pl.ds(0, OWNERS - 1)], send_sem.at[2])
        drain(fs.at[pl.ds(0, OWNERS - 1)], send_sem.at[6])
        drain(yex.at[pl.ds(0, REQS - 1)], send_sem.at[7])
        drain(obuf_like(orecv, SEQS - 1), send_sem.at[3])
        drain(frecv.at[pl.ds(0, SEQS - 1)], send_sem.at[8])

    @pl.when(jnp.logical_not(is_owner))
    def _():
        drain(obuf, send_sem.at[2])
        drain(fs, send_sem.at[6])


def obuf_like(ref, count):
    return ref.at[pl.ds(0, count), :, pl.ds(0, HEAD)]


def per_device(
    inputs, lengths, targets, cache_keys, cache_values, attention_gain, packed_weight, packed_bias, out_weight,
    feedforward_gain, gate_weight, up_weight, down_weight, final_gain, head_weight,
):
    hbm = pl.BlockSpec(memory_space=pl.ANY)
    smem = pl.BlockSpec(memory_space=pltpu.SMEM)
    vmem = pl.BlockSpec(memory_space=pltpu.VMEM)

    def held(*shape, dtype=BF16):
        return pltpu.VMEM(shape, dtype)

    return pl.pallas_call(
        kernel,
        out_shape=(
            jax.ShapeDtypeStruct((1, ROWS, PART), BF16),
            jax.ShapeDtypeStruct((1, ALL_ROWS), F32),
        ),
        in_specs=[smem, smem] + [hbm] * 13,
        out_specs=(vmem, vmem),
        scratch_shapes=[
            held(ROWS, POSITIONS * KV, HEAD),
            held(ROWS, POSITIONS * KV, HEAD),
            held(1, WIDTH, dtype=F32),
            held(PACKED_PART, WIDTH),
            held(1, PACKED_PART, dtype=F32),
            held(PART, WIDTH),
            held(1, WIDTH, dtype=F32),
            held(FF_PART, WIDTH),
            held(FF_PART, WIDTH),
            held(FF_PART, WIDTH),
            held(1, WIDTH, dtype=F32),
            held(WIDTH, VOCAB_PART),
            held(SEQS, ROWS, PART),
            held(ALL_ROWS, WIDTH, dtype=F32),
            held(ALL_ROWS, WIDTH),
            held(SEQS, ROWS, PACKED_PART),
            held(ROWS, PACKED, dtype=F32),
            held(ROWS * HEADS, HEAD, dtype=F32),
            held(ROWS * HEADS, HEAD, dtype=F32),
            held(ROWS * HEADS, HEAD, dtype=F32),
            held(ROWS * HEADS, HEAD, dtype=F32),
            held(ROWS * HEADS, HEAD, dtype=F32),
            held(OWNERS, SLAB, 2 * HEAD),
            held(SEQS, SLAB, 2 * HEAD),
            held(SEQS, SLAB, HEAD, dtype=F32),
            held(OWNERS, SLAB, HEAD),
            held(ROWS * HEADS, HEAD, dtype=F32),
            held(SEQS, REQS, ROWS, PART),
            held(OWNERS, ALL_ROWS, COLUMNS),
            held(SEQS, ALL_ROWS, COLUMNS),
            held(REQS, ALL_ROWS, COLUMNS, dtype=F32),
            held(OWNERS, ALL_ROWS, COLUMNS),
            held(REQS, 8, HEAD, dtype=F32),
            held(SEQS, 8, HEAD, dtype=F32),
            pltpu.SemaphoreType.DMA((15,)),
            pltpu.SemaphoreType.DMA((11,)),
            pltpu.SemaphoreType.DMA((11,)),
        ],
        compiler_params=pltpu.CompilerParams(
            collective_id=0, has_side_effects=True, vmem_limit_bytes=60 * 1024 * 1024
        ),
        name="decode_step",
    )(
        lengths,
        targets,
        inputs,
        cache_keys.reshape(ROWS, POSITIONS * KV, HEAD),
        cache_values.reshape(ROWS, POSITIONS * KV, HEAD),
        attention_gain.reshape(1, WIDTH),
        packed_weight.T,
        packed_bias.reshape(1, PACKED_PART),
        out_weight.T,
        feedforward_gain.reshape(1, WIDTH),
        gate_weight.T,
        up_weight.T,
        down_weight,
        final_gain.reshape(1, WIDTH),
        head_weight,
    )


def solution(mesh):
    return jax.shard_map(
        per_device,
        mesh=mesh,
        in_specs=(
            P(None, "req", "seq"),
            P("req"),
            P(),
            P("req", "seq", None, None),
            P("req", "seq", None, None),
            P(),
            P(None, "seq"),
            P("seq"),
            P(None, "seq"),
            P(),
            P(None, ("req", "seq")),
            P(None, ("req", "seq")),
            P(("req", "seq"), None),
            P(),
            P(None, ("req", "seq")),
        ),
        out_specs=(P(None, "req", "seq"), P()),
        check_vma=False,
    )
```
